512 devices in a mesh: row: 16 (over y, x), col: 32 (over z, core).
Axes of the slice: x: 4, y: 4, z: 16, core: 2. Of those that a mesh axis runs over, the one named last changes fastest.
Arguments:
- constraints: bfloat16 [2048, 8192], P(None, ('row', 'col'))
- primal: bfloat16 [2048, 2048], replicated, as said below
- dual_inv: bfloat16 [2048, 2048], replicated, as said below
- diag_shift: float32 [8192], P('row'), may hold values from 0.5 to 4
Outputs:
- trailing: float32 [8192, 8192], P('row', 'col')
- factor_cols: float32 [8192, 512], P('row')
The draws below stay inside these ranges and needn't reach their ends.
Inputs may be any that keep to these rules, and one draw needn't show every extreme that they name: `primal`: symmetric positive definite. `dual_inv`: symmetric positive definite.
All inputs are finite; a program needn't handle non-finite values.
Results may differ from the reference program's by a relative error of at most 0.0046.
Values may be sent and summed in bfloat16 or wider, within the bound.
No kernel may reach another device: no remote copies, remote signals or barrier semaphores. Data moves between devices by JAX's collectives and lax.ppermute only.
A program may use at most 128 MiB of HBM per device.

```python
import math
import jax
import jax.numpy as jnp
from jax import lax

N = 2048
PB = 256
PANELS = 2
M = 8192


def spd_matrix(key):
    normal_part = jax.random.normal(key, (N, N), jnp.float32)
    gram = jnp.dot(normal_part, normal_part.T, precision=lax.Precision.HIGHEST) / N
    return (jnp.eye(N, dtype=jnp.float32) + gram).astype(jnp.bfloat16)


def draw_primal(key, part):
    return spd_matrix(jax.random.fold_in(key, 11))


def draw_dual_inv(key, part):
    return spd_matrix(jax.random.fold_in(key, 23))


def draw_constraints(key, part):
    first_key, second_key, third_key = jax.random.split(jax.random.fold_in(key, 37), 3)
    normal_part = jax.random.normal(first_key, (N, M), jnp.float32)
    common = jax.random.normal(second_key, (N,), jnp.float32)
    loads = jax.random.uniform(third_key, (M,), jnp.float32, -1.0, 1.0)
    values = (normal_part + common[:, None] * loads[None, :]) / jnp.sqrt(jnp.float32(N))
    return values.astype(jnp.bfloat16)


def levels(key, shape, pieces, least, high):
    gain, own = 1.0, jax.random.fold_in(key, 6)
    for axis_at, parts in pieces:
        draws = jnp.exp(jax.random.uniform(jax.random.fold_in(own, axis_at), (parts,), jnp.float32, least / len(pieces), high / len(pieces)))
        gain = gain * jnp.repeat(draws, shape[axis_at] // parts).reshape([-1 if axis == axis_at else 1 for axis in range(len(shape))])
    return gain


def setup_inputs(seed: int = 0) -> dict:
    key_list = jax.random.split(jax.random.key(seed), 5)
    return {
        "constraints": draw_constraints(jax.random.fold_in(key_list[4], 71), 0),
        "primal": draw_primal(jax.random.fold_in(key_list[4], 71), 0),
        "dual_inv": draw_dual_inv(jax.random.fold_in(key_list[4], 71), 0),
        "diag_shift": jnp.clip(jnp.exp(math.log(4.0) - 2.0794415 * jax.random.uniform(key_list[3], (M,), jnp.float32) ** levels(key_list[3], (M,), ((0, 16),), -0.2, 0.2)), 0.5, 4.0),
    }


def reference(constraints, primal, dual_inv, diag_shift):
    highest = lax.Precision.HIGHEST
    cons_wide = constraints.astype(jnp.float32)
    primal_cols = jnp.dot(primal.astype(jnp.float32), cons_wide, precision=highest).astype(jnp.bfloat16)
    dual_cols = jnp.dot(dual_inv.astype(jnp.float32), cons_wide, precision=highest).astype(jnp.bfloat16)
    gram_primal = jnp.dot(cons_wide.T, primal_cols.astype(jnp.float32), precision=highest)
    gram_dual = jnp.dot(cons_wide.T, dual_cols.astype(jnp.float32), precision=highest)
    schur = gram_primal * gram_dual + jnp.diag(diag_shift)
    positions = jnp.arange(M)
    panels = []
    for panel_index in range(PANELS):
        first = panel_index * PB
        pivot = jnp.linalg.cholesky(schur[first:first + PB, first:first + PB])
        column_panel = schur[:, first:first + PB]
        lower_part = jax.scipy.linalg.solve_triangular(pivot, column_panel.T, lower=True).T
        lower_part = jnp.where((positions >= first)[:, None], lower_part, jnp.float32(0.0))
        schur = schur - jnp.dot(lower_part, lower_part.T, precision=highest)
        panels.append(lower_part)
    return (schur, jnp.concatenate(panels, axis=1))
```

```python
import jax
import jax.numpy as jnp
from jax import lax
from jax.sharding import PartitionSpec as P

PB = 256
PANELS = 2
LANES = 128


def nt(left, right, precision=None):
    return lax.dot_general(
        left,
        right,
        (((1,), (1,)), ((), ())),
        precision=precision,
        preferred_element_type=jnp.float32,
    )


def exchange(value, axis):
    return lax.all_to_all(value, axis, split_axis=0, concat_axis=0, tiled=True)


def split_three(value):
    high = value.astype(jnp.bfloat16)
    rest = value - high.astype(jnp.float32)
    middle = rest.astype(jnp.bfloat16)
    low = (rest - middle.astype(jnp.float32)).astype(jnp.bfloat16)
    return high, middle, low


def factor(panel_block):
    highest = lax.Precision.HIGHEST
    eye = jnp.eye(PB, dtype=jnp.float32)
    s00 = panel_block[:PB, :PB]
    s10 = panel_block[PB:, :PB]
    s11 = panel_block[PB:, PB:]
    pivot0 = jnp.linalg.cholesky(s00)
    inv0 = jax.scipy.linalg.solve_triangular(pivot0, eye, lower=True)
    l10 = nt(s10, inv0, highest)
    pivot1 = jnp.linalg.cholesky(s11 - nt(l10, l10, highest))
    inv1 = jax.scipy.linalg.solve_triangular(pivot1, eye, lower=True)
    inv10 = -jnp.dot(
        jnp.dot(inv1, l10, precision=highest), inv0, precision=highest
    )
    top = jnp.concatenate([inv0, jnp.zeros_like(inv0)], axis=1)
    return jnp.concatenate([top, jnp.concatenate([inv10, inv1], axis=1)], axis=0)


def local(constraints, primal, dual_inv, diag_shift):
    n_row = lax.axis_size("row")
    n_col = lax.axis_size("col")
    row_place = lax.axis_index("row")
    col_place = lax.axis_index("col")
    depth, own = constraints.shape
    blocks = depth // LANES
    wide = PB * PANELS
    local_rows = own * n_col
    local_cols = own * n_row
    half = local_rows // 2

    cons = constraints.T
    cons_rows = lax.all_gather(cons, "col", axis=0, tiled=True)

    moves = [
        ((c // 2) * n_col + (c % 2) * n_row + r, r * n_col + c)
        for r in range(n_row)
        for c in range(n_col)
    ]
    moved = lax.ppermute(cons, ("row", "col"), moves)

    parts = cons.reshape(own, blocks, LANES).transpose(1, 0, 2)
    shift = jnp.concatenate([x.reshape(-1, LANES) for x in split_three(diag_shift)], axis=0)
    shift = jnp.pad(shift, ((0, own - shift.shape[0]), (0, 0)))
    first = jnp.concatenate([parts, jnp.broadcast_to(shift, (blocks, own, LANES))], axis=1)
    first = exchange(first, "row")[0]
    shift = first[own : own + 3 * local_rows // LANES].astype(jnp.float32)
    shift = shift.reshape(3, local_rows)
    panel_shift = shift[0] + shift[1] + shift[2]
    every = exchange(jnp.broadcast_to(first[:own], (n_col, own, LANES)), "col")
    every = every.reshape(local_rows, LANES)

    core = col_place % 2
    mine = lax.dynamic_slice_in_dim(every, core * half, half, 0)
    moved = moved.reshape(own, blocks, LANES).transpose(1, 0, 2).reshape(own * blocks, LANES)
    both = jnp.concatenate([mine, moved], axis=0)
    both = exchange(jnp.broadcast_to(both, (n_row,) + both.shape), "row")
    mine = both[:, :half].transpose(1, 0, 2).reshape(half, depth)
    other = lax.ppermute(mine, "col", [(c, c ^ 1) for c in range(n_col)])
    cons_panel = jnp.concatenate(
        [jnp.where(core == 0, mine, other), jnp.where(core == 0, other, mine)], axis=0
    )
    cons_cols = both[:, half:].reshape(n_row, blocks, own, LANES)
    cons_cols = cons_cols.transpose(0, 2, 1, 3).reshape(local_cols, depth)

    panel_primal = nt(cons_panel, primal).astype(jnp.bfloat16)
    panel_dual = nt(cons_panel, dual_inv).astype(jnp.bfloat16)
    panel_ids = jnp.arange(wide, dtype=jnp.int32)
    shift_block = jnp.where(
        panel_ids[:, None] == panel_ids[None, :], panel_shift[None, :], jnp.float32(0.0)
    )
    panel_block = (
        nt(cons_panel, panel_primal) * nt(cons_panel, panel_dual) + shift_block
    )
    inverse = factor(panel_block)

    col_primal = nt(cons_cols, primal).astype(jnp.bfloat16)
    col_dual = nt(cons_cols, dual_inv).astype(jnp.bfloat16)
    global_rows = row_place * local_rows + jnp.arange(local_rows, dtype=jnp.int32)
    global_cols = col_place * local_cols + jnp.arange(local_cols, dtype=jnp.int32)

    def panel_rows(cons_part, ids):
        block = nt(cons_part, panel_primal) * nt(cons_part, panel_dual) + jnp.where(
            ids[:, None] == panel_ids[None, :], panel_shift[None, :], jnp.float32(0.0)
        )
        rows = nt(block, inverse, lax.Precision.HIGHEST)
        return jnp.where(
            ids[:, None] >= (panel_ids // PB * PB)[None, :], rows, jnp.float32(0.0)
        )

    col_factor = panel_rows(cons_cols, global_cols)
    row_factor = panel_rows(cons_rows, global_rows)
    schur = nt(cons_rows, col_primal) * nt(cons_rows, col_dual) + jnp.where(
        global_rows[:, None] == global_cols[None, :], diag_shift[:, None], jnp.float32(0.0)
    )
    trailing = schur - nt(row_factor, col_factor, lax.Precision.HIGHEST)
    return (trailing, row_factor)


def solution(mesh):
    return jax.shard_map(
        local,
        mesh=mesh,
        in_specs=(P(None, ("row", "col")), P(), P(), P("row")),
        out_specs=(P("row", "col"), P("row", None)),
        check_vma=False,
    )
```

```python
import jax
import jax.numpy as jnp
from jax import lax
from jax.experimental import pallas as pl
from jax.experimental.pallas import tpu as pltpu
from jax.sharding import PartitionSpec as P

PB = 256
PANELS = 2
LANES = 128
SUB = 8
HIGHEST = lax.Precision.HIGHEST


def nt(left, right, precision=None):
    return lax.dot_general(
        left,
        right,
        (((1,), (1,)), ((), ())),
        precision=precision,
        preferred_element_type=jnp.float32,
    )


def dot_full(left, right):
    return jnp.dot(left, right, precision=HIGHEST, preferred_element_type=jnp.float32)


def exchange(value, axis):
    return lax.all_to_all(value, axis, split_axis=0, concat_axis=0, tiled=True)


def split_three(value):
    high = value.astype(jnp.bfloat16)
    rest = value - high.astype(jnp.float32)
    middle = rest.astype(jnp.bfloat16)
    low = (rest - middle.astype(jnp.float32)).astype(jnp.bfloat16)
    return high, middle, low


def spread_lane(value, at):
    return jnp.broadcast_to(value[:, at : at + 1], (SUB, LANES))


def spread_row(value, at):
    return jnp.broadcast_to(value[at : at + 1, :], (SUB, LANES))


def tree_sum(terms):
    while len(terms) > 1:
        paired = [a + b for a, b in zip(terms[::2], terms[1::2])]
        terms = paired + terms[len(terms) // 2 * 2 :]
    return terms[0]


def eliminate(work):
    row = lax.broadcasted_iota(jnp.int32, (SUB, LANES), 0)
    steps = LANES // SUB
    for step in range(steps):
        low = step * SUB
        here = slice(low, low + SUB)
        left = work[here, :LANES]
        right = work[here, LANES:]
        inv = [spread_lane(left, low + k) for k in range(SUB)]
        forward = [jnp.where(row == k, 1.0, 0.0) for k in range(SUB)]
        scale = None
        for i in range(SUB):
            pivot = spread_row(inv[i], i)
            recip = 1.0 / pivot
            root = lax.rsqrt(pivot)
            scale = root if scale is None else jnp.where(row == i, root, scale)
            ratio = inv[i] * recip
            below = jnp.where(row > i, ratio, 0.0)
            for k in range(i + 1):
                forward[k] = forward[k] - below * spread_row(forward[k], i)
            updated = []
            for k in range(SUB):
                if k == i:
                    updated.append(jnp.where(row == i, recip, -ratio))
                else:
                    across = spread_row(inv[k], i)
                    updated.append(
                        jnp.where(row == i, across * recip, inv[k] - ratio * across)
                    )
            inv = updated
        right_rows = [spread_row(right, k) for k in range(SUB)]
        if step + 1 < steps:
            left_rows = [spread_row(left, k) for k in range(SUB)]
            solved_left = tree_sum([inv[k] * left_rows[k] for k in range(SUB)])
            solved_right = tree_sum([inv[k] * right_rows[k] for k in range(SUB)])
            left_terms = [spread_row(solved_left, k) for k in range(SUB)]
            right_terms = [spread_row(solved_right, k) for k in range(SUB)]
            for later in range(step + 1, steps):
                there = slice(later * SUB, later * SUB + SUB)
                current = work[there, :LANES]
                weights = [spread_lane(current, low + k) for k in range(SUB)]
                work[there, :LANES] = current - tree_sum(
                    [weights[k] * left_terms[k] for k in range(SUB)]
                )
                work[there, LANES:] = work[there, LANES:] - tree_sum(
                    [weights[k] * right_terms[k] for k in range(SUB)]
                )
        work[here, LANES:] = scale * tree_sum(
            [forward[k] * right_rows[k] for k in range(SUB)]
        )


def factor_kernel(block, inverse, rest, work):
    size = block.shape[0]
    row = lax.broadcasted_iota(jnp.int32, (LANES, LANES), 0)
    lane = lax.broadcasted_iota(jnp.int32, (LANES, LANES), 1)
    eye = jnp.where(row == lane, 1.0, 0.0).astype(jnp.float32)
    for panel in range(PANELS):
        at = slice(panel * PB, (panel + 1) * PB)
        pivot = block[at, at]
        rest[at, at] = 0.5 * (pivot + pivot.T)
        for later in range(panel + 1, PANELS):
            below = slice(later * PB, (later + 1) * PB)
            rest[at, below] = block[below, at].T
    inverse[...] = jnp.zeros_like(inverse)

    def load(low):
        work[:, :LANES] = rest[low : low + LANES, low : low + LANES]

    def update(low):
        high = low + LANES
        own = work[:, LANES:]
        if low:
            inverse[low:high, :low] = dot_full(own, inverse[low:high, :low])
        inverse[low:high, low:high] = own
        if high < size:
            upper = dot_full(own, rest[low:high, high:])
            lower = upper.T
            rest[high:, high:] = rest[high:, high:] - dot_full(lower, upper)
            inverse[high:, :high] = inverse[high:, :high] - dot_full(
                lower, inverse[low:high, :high]
            )

    @pl.loop(0, size // LANES)
    def _(block_index):
        for index in range(size // LANES):
            pl.when(block_index == index)(lambda: load(index * LANES))
        work[:, LANES:] = eye
        eliminate(work)
        for index in range(size // LANES):
            pl.when(block_index == index)(lambda: update(index * LANES))


def factor(block):
    size = block.shape[0]
    return pl.pallas_call(
        factor_kernel,
        out_shape=jax.ShapeDtypeStruct((size, size), jnp.float32),
        in_specs=[pl.BlockSpec(memory_space=pltpu.VMEM)],
        out_specs=pl.BlockSpec(memory_space=pltpu.VMEM),
        scratch_shapes=[
            pltpu.VMEM((size, size), jnp.float32),
            pltpu.VMEM((LANES, 2 * LANES), jnp.float32),
        ],
        name="factor",
    )(block)


def local(constraints, primal, dual_inv, diag_shift):
    n_row = lax.axis_size("row")
    n_col = lax.axis_size("col")
    row_place = lax.axis_index("row")
    col_place = lax.axis_index("col")
    depth, own = constraints.shape
    blocks = depth // LANES
    wide = PB * PANELS
    local_rows = own * n_col
    local_cols = own * n_row
    half = local_rows // 2
    core = col_place % 2

    cons = constraints.T
    cons_rows = lax.all_gather(cons, "col", axis=0, tiled=True)

    parts = cons.reshape(own, blocks, LANES).transpose(1, 0, 2)
    shift = jnp.concatenate([x.reshape(-1, LANES) for x in split_three(diag_shift)], axis=0)
    shift = jnp.pad(shift, ((0, own - shift.shape[0]), (0, 0)))
    first = jnp.concatenate([parts, jnp.broadcast_to(shift, (blocks, own, LANES))], axis=1)
    first = exchange(first, "row")
    shift = first[0, own : own + 3 * local_rows // LANES].astype(jnp.float32)
    shift = shift.reshape(3, local_rows)
    panel_shift = shift[0] + shift[1] + shift[2]

    first = first[:, :own]
    second = jnp.concatenate(
        [
            jnp.broadcast_to(first[0], (n_col, own, LANES)),
            jnp.repeat(first, n_col // n_row, axis=0),
        ],
        axis=1,
    )
    second = exchange(second, "col")

    third = lax.dynamic_slice_in_dim(second, core * n_row, n_row, 0)
    third = exchange(jnp.broadcast_to(third, (n_row,) + third.shape), "row")
    third = third.transpose(1, 2, 0, 3)
    mine = third[:, :own].reshape(half, depth)
    cons_cols = third[:, own:].reshape(local_cols, depth)
    other = lax.ppermute(mine, "col", [(c, c ^ 1) for c in range(n_col)])
    cons_every = jnp.concatenate(
        [jnp.where(core == 0, mine, other), jnp.where(core == 0, other, mine), cons_cols],
        axis=0,
    )

    every_primal = nt(cons_every, primal).astype(jnp.bfloat16)
    every_dual = nt(cons_every, dual_inv).astype(jnp.bfloat16)
    panel_primal, col_primal = every_primal[:wide], every_primal[wide:]
    panel_dual, col_dual = every_dual[:wide], every_dual[wide:]
    panel_ids = jnp.arange(wide, dtype=jnp.int32)

    def panel_columns(cons_part, ids):
        return nt(cons_part, panel_primal) * nt(cons_part, panel_dual) + jnp.where(
            ids[:, None] == panel_ids[None, :], panel_shift[None, :], jnp.float32(0.0)
        )

    def panel_rows(cons_part, ids):
        rows = nt(panel_columns(cons_part, ids), inverse, HIGHEST)
        return jnp.where(
            ids[:, None] >= (panel_ids // PB * PB)[None, :], rows, jnp.float32(0.0)
        )

    inverse = factor(panel_columns(cons_every[:wide], panel_ids))
    global_rows = row_place * local_rows + jnp.arange(local_rows, dtype=jnp.int32)
    global_cols = col_place * local_cols + jnp.arange(local_cols, dtype=jnp.int32)
    col_factor = panel_rows(cons_cols, global_cols)
    row_factor = panel_rows(cons_rows, global_rows)
    schur = nt(cons_rows, col_primal) * nt(cons_rows, col_dual) + jnp.where(
        global_rows[:, None] == global_cols[None, :], diag_shift[:, None], jnp.float32(0.0)
    )
    trailing = schur - nt(row_factor, col_factor, HIGHEST)
    return (trailing, row_factor)


def solution(mesh):
    return jax.shard_map(
        local,
        mesh=mesh,
        in_specs=(P(None, ("row", "col")), P(), P(), P("row")),
        out_specs=(P("row", "col"), P("row", None)),
        check_vma=False,
    )
```

```python
import functools

import jax
import jax.numpy as jnp
from jax import lax
from jax.experimental import pallas as pl
from jax.experimental.pallas import tpu as pltpu
from jax.sharding import PartitionSpec as P

PB = 256
PANELS = 2
LANES = 128
SUB = 8
HIGHEST = lax.Precision.HIGHEST

VMEM_BYTES = 60 * 1024 * 1024


def nt(left, right, precision=None):
    return lax.dot_general(
        left,
        right,
        (((1,), (1,)), ((), ())),
        precision=precision,
        preferred_element_type=jnp.float32,
    )


def dot_full(left, right):
    return jnp.dot(left, right, precision=HIGHEST, preferred_element_type=jnp.float32)


def exchange(value, axis):
    return lax.all_to_all(value, axis, split_axis=0, concat_axis=0, tiled=True)


def split_three(value):
    high = value.astype(jnp.bfloat16)
    rest = value - high.astype(jnp.float32)
    middle = rest.astype(jnp.bfloat16)
    low = (rest - middle.astype(jnp.float32)).astype(jnp.bfloat16)
    return high, middle, low


def spread_lane(value, at):
    return jnp.broadcast_to(value[:, at : at + 1], (SUB, LANES))


def spread_row(value, at):
    return jnp.broadcast_to(value[at : at + 1, :], (SUB, LANES))


def tree_sum(terms):
    while len(terms) > 1:
        paired = [a + b for a, b in zip(terms[::2], terms[1::2])]
        terms = paired + terms[len(terms) // 2 * 2 :]
    return terms[0]


def eliminate(work):
    row = lax.broadcasted_iota(jnp.int32, (SUB, LANES), 0)
    steps = LANES // SUB
    for step in range(steps):
        low = step * SUB
        here = slice(low, low + SUB)
        left = work[here, :LANES]
        right = work[here, LANES:]
        inv = [spread_lane(left, low + k) for k in range(SUB)]
        forward = [jnp.where(row == k, 1.0, 0.0) for k in range(SUB)]
        scale = None
        for i in range(SUB):
            pivot = spread_row(inv[i], i)
            recip = 1.0 / pivot
            root = lax.rsqrt(pivot)
            scale = root if scale is None else jnp.where(row == i, root, scale)
            ratio = inv[i] * recip
            below = jnp.where(row > i, ratio, 0.0)
            for k in range(i + 1):
                forward[k] = forward[k] - below * spread_row(forward[k], i)
            updated = []
            for k in range(SUB):
                if k == i:
                    updated.append(jnp.where(row == i, recip, -ratio))
                else:
                    across = spread_row(inv[k], i)
                    updated.append(
                        jnp.where(row == i, across * recip, inv[k] - ratio * across)
                    )
            inv = updated
        right_rows = [spread_row(right, k) for k in range(SUB)]
        if step + 1 < steps:
            left_rows = [spread_row(left, k) for k in range(SUB)]
            solved_left = tree_sum([inv[k] * left_rows[k] for k in range(SUB)])
            solved_right = tree_sum([inv[k] * right_rows[k] for k in range(SUB)])
            left_terms = [spread_row(solved_left, k) for k in range(SUB)]
            right_terms = [spread_row(solved_right, k) for k in range(SUB)]
            for later in range(step + 1, steps):
                there = slice(later * SUB, later * SUB + SUB)
                current = work[there, :LANES]
                weights = [spread_lane(current, low + k) for k in range(SUB)]
                work[there, :LANES] = current - tree_sum(
                    [weights[k] * left_terms[k] for k in range(SUB)]
                )
                work[there, LANES:] = work[there, LANES:] - tree_sum(
                    [weights[k] * right_terms[k] for k in range(SUB)]
                )
        work[here, LANES:] = scale * tree_sum(
            [forward[k] * right_rows[k] for k in range(SUB)]
        )


def factor_block(block, inverse, rest, work):
    size = block.shape[0]
    row = lax.broadcasted_iota(jnp.int32, (LANES, LANES), 0)
    lane = lax.broadcasted_iota(jnp.int32, (LANES, LANES), 1)
    eye = jnp.where(row == lane, 1.0, 0.0).astype(jnp.float32)
    for panel in range(PANELS):
        at = slice(panel * PB, (panel + 1) * PB)
        pivot = block[at, at]
        rest[at, at] = 0.5 * (pivot + pivot.T)
        for later in range(panel + 1, PANELS):
            below = slice(later * PB, (later + 1) * PB)
            rest[at, below] = block[below, at].T
    inverse[...] = jnp.zeros_like(inverse)

    def load(low):
        work[:, :LANES] = rest[low : low + LANES, low : low + LANES]

    def update(low):
        high = low + LANES
        own = work[:, LANES:]
        if low:
            inverse[low:high, :low] = dot_full(own, inverse[low:high, :low])
        inverse[low:high, low:high] = own
        if high < size:
            upper = dot_full(own, rest[low:high, high:])
            lower = upper.T
            rest[high:, high:] = rest[high:, high:] - dot_full(lower, upper)
            inverse[high:, :high] = inverse[high:, :high] - dot_full(
                lower, inverse[low:high, :high]
            )

    @pl.loop(0, size // LANES)
    def _(block_index):
        for index in range(size // LANES):
            pl.when(block_index == index)(lambda: load(index * LANES))
        work[:, LANES:] = eye
        eliminate(work)
        for index in range(size // LANES):
            pl.when(block_index == index)(lambda: update(index * LANES))


def panel_shift(parts):
    count = PB * PANELS // LANES
    wide = parts[...].astype(jnp.float32)
    wide = wide[:count] + wide[count : 2 * count] + wide[2 * count : 3 * count]
    return jnp.concatenate([wide[k : k + 1] for k in range(count)], axis=1)


def on_panel(shape, start, shift):
    row = lax.broadcasted_iota(jnp.int32, shape, 0) + start
    lane = lax.broadcasted_iota(jnp.int32, shape, 1)
    return jnp.where(row == lane, jnp.broadcast_to(shift, shape), 0.0)


def from_panel(rows, start):
    row = lax.broadcasted_iota(jnp.int32, rows.shape, 0) + start
    lane = lax.broadcasted_iota(jnp.int32, rows.shape, 1)
    return jnp.where(row >= lane // PB * PB, rows, 0.0)


def front_kernel(
    places,
    gathered,
    other,
    parts,
    primal,
    dual,
    primal_out,
    dual_out,
    inverse,
    col_factor,
    matrix,
    every,
    every_primal,
    every_dual,
    block,
    rest,
    work,
    sems,
    out_sems,
):
    wide = PB * PANELS
    chunks = matrix.shape[1]
    size = matrix.shape[2]
    core, _, col_start = places()
    sources = (primal, dual)
    results = (every_primal, every_dual)

    def fetch(which, chunk):
        return pltpu.make_async_copy(
            sources[which].at[pl.ds(chunk * size, size)],
            matrix.at[which, chunk],
            sems.at[which, chunk],
        )

    for which in range(2):
        for chunk in range(chunks):
            fetch(which, chunk).start()

    blocks = gathered.shape[0]
    own = other.shape[2]
    half = other.shape[1] * own
    mine_at = pl.multiple_of(core * half, half)
    other_at = pl.multiple_of((1 - core) * half, half)
    for b in range(blocks):
        lanes = slice(b * LANES, (b + 1) * LANES)
        every[pl.ds(mine_at, half), lanes] = gathered[b, :, :own, :].reshape(half, LANES)
        every[pl.ds(other_at, half), lanes] = other[b].reshape(half, LANES)
        every[wide:, lanes] = gathered[b, :, own:, :].reshape(-1, LANES)

    for which in range(2):

        @pl.loop(0, chunks)
        def _(chunk):
            fetch(which, chunk).wait()
            at = pl.multiple_of(chunk * size, size)
            results[which][:, pl.ds(at, size)] = nt(
                every[...], matrix[which, chunk]
            ).astype(jnp.bfloat16)

    sends = [
        pltpu.make_async_copy(every_primal, primal_out, out_sems.at[0]),
        pltpu.make_async_copy(every_dual, dual_out, out_sems.at[1]),
    ]
    for send in sends:
        send.start()

    shift = panel_shift(parts)
    panel_primal = every_primal[:wide, :]
    panel_dual = every_dual[:wide, :]
    products = nt(every[...], panel_primal) * nt(every[...], panel_dual)
    block[...] = products[:wide] + on_panel((wide, wide), 0, shift)
    columns = products[wide:] + on_panel((products.shape[0] - wide, wide), col_start, shift)
    factor_block(block, inverse, rest, work)
    col_factor[...] = from_panel(nt(columns, inverse[...], HIGHEST), col_start)
    for send in sends:
        send.wait()


def front(places, gathered, other, parts, primal, dual):
    wide = PB * PANELS
    depth = primal.shape[0]
    cols = gathered.shape[1] * (gathered.shape[2] - other.shape[2])
    chunks = 4
    bf16 = jnp.bfloat16
    in_vmem = pl.BlockSpec(memory_space=pltpu.VMEM)
    in_place = pl.BlockSpec(memory_space=pl.ANY)
    return pl.pallas_call(
        functools.partial(front_kernel, places),
        out_shape=(
            jax.ShapeDtypeStruct((wide + cols, depth), bf16),
            jax.ShapeDtypeStruct((wide + cols, depth), bf16),
            jax.ShapeDtypeStruct((wide, wide), jnp.float32),
            jax.ShapeDtypeStruct((cols, wide), jnp.float32),
        ),
        in_specs=[in_vmem, in_vmem, in_vmem, in_place, in_place],
        out_specs=(in_place, in_place, in_vmem, in_vmem),
        scratch_shapes=[
            pltpu.VMEM((2, chunks, depth // chunks, depth), bf16),
            pltpu.VMEM((wide + cols, depth), bf16),
            pltpu.VMEM((wide + cols, depth), bf16),
            pltpu.VMEM((wide + cols, depth), bf16),
            pltpu.VMEM((wide, wide), jnp.float32),
            pltpu.VMEM((wide, wide), jnp.float32),
            pltpu.VMEM((LANES, 2 * LANES), jnp.float32),
            pltpu.SemaphoreType.DMA((2, chunks)),
            pltpu.SemaphoreType.DMA((2,)),
        ],
        compiler_params=pltpu.CompilerParams(vmem_limit_bytes=VMEM_BYTES),
        name="front",
    )(gathered, other, parts, primal, dual)


def back_kernel(
    places,
    rows_in,
    primal_in,
    dual_in,
    inverse_in,
    col_factor,
    parts,
    shift_row,
    trailing,
    row_factor,
    rows,
    every_primal,
    every_dual,
    inverse,
    sems,
):
    wide = PB * PANELS
    _, row_start, col_start = places()
    panel, column = slice(0, wide), slice(wide, None)
    copies = [
        pltpu.make_async_copy(source, target, sems.at[k])
        for k, (source, target) in enumerate(
            [
                (rows_in, rows),
                (primal_in.at[panel], every_primal.at[panel]),
                (dual_in.at[panel], every_dual.at[panel]),
                (inverse_in, inverse),
                (primal_in.at[column], every_primal.at[column]),
                (dual_in.at[column], every_dual.at[column]),
            ]
        )
    ]
    for copy in copies:
        copy.start()
    shift = panel_shift(parts)
    count = rows.shape[0]
    own_shift = jnp.sum(on_panel((count, count), 0, shift_row[...]), axis=1, keepdims=True)
    for copy in copies[:2]:
        copy.wait()
    first = nt(rows[...], every_primal[panel, :])
    copies[2].wait()
    products = first * nt(rows[...], every_dual[panel, :])
    products = products + on_panel((count, wide), row_start, shift)
    copies[3].wait()
    factor = from_panel(nt(products, inverse[...], HIGHEST), row_start)
    row_factor[...] = factor
    for copy in copies[4:]:
        copy.wait()
    schur = nt(rows[...], every_primal[column, :]) * nt(rows[...], every_dual[column, :])
    row = lax.broadcasted_iota(jnp.int32, schur.shape, 0) + row_start
    lane = lax.broadcasted_iota(jnp.int32, schur.shape, 1) + col_start
    schur = schur + jnp.where(row == lane, jnp.broadcast_to(own_shift, schur.shape), 0.0)
    trailing[...] = schur - nt(factor, col_factor[...], HIGHEST)


def back(places, rows, primal, dual, inverse, col_factor, parts, shift_row):
    wide = PB * PANELS
    count, depth = rows.shape
    cols = col_factor.shape[0]
    bf16 = jnp.bfloat16
    in_vmem = pl.BlockSpec(memory_space=pltpu.VMEM)
    in_place = pl.BlockSpec(memory_space=pl.ANY)
    return pl.pallas_call(
        functools.partial(back_kernel, places),
        out_shape=(
            jax.ShapeDtypeStruct((count, cols), jnp.float32),
            jax.ShapeDtypeStruct((count, wide), jnp.float32),
        ),
        in_specs=[in_place] * 4 + [in_vmem] * 3,
        out_specs=(in_vmem, in_vmem),
        scratch_shapes=[
            pltpu.VMEM((count, depth), bf16),
            pltpu.VMEM((wide + cols, depth), bf16),
            pltpu.VMEM((wide + cols, depth), bf16),
            pltpu.VMEM((wide, wide), jnp.float32),
            pltpu.SemaphoreType.DMA((6,)),
        ],
        compiler_params=pltpu.CompilerParams(vmem_limit_bytes=VMEM_BYTES),
        name="back",
    )(rows, primal, dual, inverse, col_factor, parts, shift_row)


def local(constraints, primal, dual_inv, diag_shift):
    n_row = lax.axis_size("row")
    n_col = lax.axis_size("col")
    depth, own = constraints.shape
    blocks = depth // LANES
    local_rows = own * n_col
    local_cols = own * n_row

    def places():
        col_place = lax.axis_index("col")
        return col_place % 2, lax.axis_index("row") * local_rows, col_place * local_cols

    cons = constraints.T

    parts = cons.reshape(own, blocks, LANES).transpose(1, 0, 2)
    shift = jnp.concatenate([x.reshape(-1, LANES) for x in split_three(diag_shift)], axis=0)
    shift = jnp.pad(shift, ((0, own - shift.shape[0]), (0, 0)))
    first = jnp.concatenate([parts, jnp.broadcast_to(shift, (blocks, own, LANES))], axis=1)
    first = exchange(first, "row")
    shift = first[0, own:]

    first = first[:, :own]
    second = jnp.concatenate(
        [
            jnp.broadcast_to(first[0], (n_col, own, LANES)),
            jnp.repeat(first, n_col // n_row, axis=0),
        ],
        axis=1,
    )
    second = exchange(second, "col")

    second, cons = lax.optimization_barrier((second, cons))
    cons_rows = lax.all_gather(cons, "col", axis=0, tiled=True)

    third = lax.dynamic_slice_in_dim(second, lax.axis_index("col") % 2 * n_row, n_row, 0)
    third = exchange(jnp.broadcast_to(third, (n_row,) + third.shape), "row")
    other = lax.ppermute(third[:, :, :own], "col", [(c, c ^ 1) for c in range(n_col)])

    every_primal, every_dual, inverse, col_factor = front(
        places, third, other, shift, primal, dual_inv
    )
    return back(
        places,
        cons_rows,
        every_primal,
        every_dual,
        inverse,
        col_factor,
        shift,
        diag_shift.reshape(1, -1),
    )


def solution(mesh):
    return jax.shard_map(
        local,
        mesh=mesh,
        in_specs=(P(None, ("row", "col")), P(), P(), P("row")),
        out_specs=(P("row", "col"), P("row", None)),
        check_vma=False,
    )
```

```python
import functools

import jax
import jax.numpy as jnp
from jax import lax
from jax.experimental import pallas as pl
from jax.experimental.pallas import tpu as pltpu
from jax.sharding import PartitionSpec as P

PB = 256
PANELS = 2
LANES = 128
SUB = 8
HIGHEST = lax.Precision.HIGHEST

VMEM_BYTES = 60 * 1024 * 1024


def nt(left, right, precision=None):
    return lax.dot_general(
        left,
        right,
        (((1,), (1,)), ((), ())),
        precision=precision,
        preferred_element_type=jnp.float32,
    )


def dot_full(left, right):
    return jnp.dot(left, right, precision=HIGHEST, preferred_element_type=jnp.float32)


def exchange(value, axis):
    return lax.all_to_all(value, axis, split_axis=0, concat_axis=0, tiled=True)


def split_three(value):
    high = value.astype(jnp.bfloat16)
    rest = value - high.astype(jnp.float32)
    middle = rest.astype(jnp.bfloat16)
    low = (rest - middle.astype(jnp.float32)).astype(jnp.bfloat16)
    return high, middle, low


def spread_lane(value, at):
    return jnp.broadcast_to(value[:, at : at + 1], (SUB, LANES))


def spread_row(value, at):
    return jnp.broadcast_to(value[at : at + 1, :], (SUB, LANES))


def tree_sum(terms):
    while len(terms) > 1:
        paired = [a + b for a, b in zip(terms[::2], terms[1::2])]
        terms = paired + terms[len(terms) // 2 * 2 :]
    return terms[0]


def eliminate(work):
    row = lax.broadcasted_iota(jnp.int32, (SUB, LANES), 0)
    steps = LANES // SUB
    for step in range(steps):
        low = step * SUB
        here = slice(low, low + SUB)
        left = work[here, :LANES]
        right = work[here, LANES:]
        inv = [spread_lane(left, low + k) for k in range(SUB)]
        forward = [jnp.where(row == k, 1.0, 0.0) for k in range(SUB)]
        scale = None
        for i in range(SUB):
            pivot = spread_row(inv[i], i)
            recip = 1.0 / pivot
            root = lax.rsqrt(pivot)
            scale = root if scale is None else jnp.where(row == i, root, scale)
            ratio = inv[i] * recip
            below = jnp.where(row > i, ratio, 0.0)
            for k in range(i + 1):
                forward[k] = forward[k] - below * spread_row(forward[k], i)
            updated = []
            for k in range(SUB):
                if k == i:
                    updated.append(jnp.where(row == i, recip, -ratio))
                else:
                    across = spread_row(inv[k], i)
                    updated.append(
                        jnp.where(row == i, across * recip, inv[k] - ratio * across)
                    )
            inv = updated
        right_rows = [spread_row(right, k) for k in range(SUB)]
        if step + 1 < steps:
            left_rows = [spread_row(left, k) for k in range(SUB)]
            solved_left = tree_sum([inv[k] * left_rows[k] for k in range(SUB)])
            solved_right = tree_sum([inv[k] * right_rows[k] for k in range(SUB)])
            left_terms = [spread_row(solved_left, k) for k in range(SUB)]
            right_terms = [spread_row(solved_right, k) for k in range(SUB)]
            for later in range(step + 1, steps):
                there = slice(later * SUB, later * SUB + SUB)
                current = work[there, :LANES]
                weights = [spread_lane(current, low + k) for k in range(SUB)]
                work[there, :LANES] = current - tree_sum(
                    [weights[k] * left_terms[k] for k in range(SUB)]
                )
                work[there, LANES:] = work[there, LANES:] - tree_sum(
                    [weights[k] * right_terms[k] for k in range(SUB)]
                )
        work[here, LANES:] = scale * tree_sum(
            [forward[k] * right_rows[k] for k in range(SUB)]
        )


def factor_block(block, inverse, rest, work, beside):
    size = block.shape[0]
    row = lax.broadcasted_iota(jnp.int32, (LANES, LANES), 0)
    lane = lax.broadcasted_iota(jnp.int32, (LANES, LANES), 1)
    eye = jnp.where(row == lane, 1.0, 0.0).astype(jnp.float32)
    for panel in range(PANELS):
        at = slice(panel * PB, (panel + 1) * PB)
        pivot = block[at, at]
        rest[at, at] = 0.5 * (pivot + pivot.T)
        for later in range(panel + 1, PANELS):
            below = slice(later * PB, (later + 1) * PB)
            rest[at, below] = block[below, at].T
    inverse[...] = jnp.zeros_like(inverse)

    def load(low):
        work[:, :LANES] = rest[low : low + LANES, low : low + LANES]

    def update(low):
        high = low + LANES
        own = work[:, LANES:]
        if low:
            inverse[low:high, :low] = dot_full(own, inverse[low:high, :low])
        inverse[low:high, low:high] = own
        if high < size:
            upper = dot_full(own, rest[low:high, high:])
            lower = upper.T
            rest[high:, high:] = rest[high:, high:] - dot_full(lower, upper)
            inverse[high:, :high] = inverse[high:, :high] - dot_full(
                lower, inverse[low:high, :high]
            )

    @pl.loop(0, size // LANES)
    def _(block_index):
        for index in range(size // LANES):
            pl.when(block_index == index)(lambda: load(index * LANES))
        work[:, LANES:] = eye
        beside(block_index)
        eliminate(work)
        for index in range(size // LANES):
            pl.when(block_index == index)(lambda: update(index * LANES))


def panel_shift(parts):
    count = PB * PANELS // LANES
    wide = parts[...].astype(jnp.float32)
    wide = wide[:count] + wide[count : 2 * count] + wide[2 * count : 3 * count]
    return jnp.concatenate([wide[k : k + 1] for k in range(count)], axis=1)


def on_panel(shape, start, shift):
    row = lax.broadcasted_iota(jnp.int32, shape, 0) + start
    lane = lax.broadcasted_iota(jnp.int32, shape, 1)
    return jnp.where(row == lane, jnp.broadcast_to(shift, shape), 0.0)


def from_panel(rows, start):
    row = lax.broadcasted_iota(jnp.int32, rows.shape, 0) + start
    lane = lax.broadcasted_iota(jnp.int32, rows.shape, 1)
    return jnp.where(row >= lane // PB * PB, rows, 0.0)


def whole_kernel(
    places,
    gathered_in,
    other_in,
    rows_in,
    parts,
    shift_row,
    primal,
    dual,
    trailing,
    row_factor,
    gathered,
    other,
    rows,
    matrix,
    every,
    every_primal,
    every_dual,
    block,
    rest,
    inverse,
    work,
    row_products,
    col_products,
    sems,
    in_sems,
):
    wide = PB * PANELS
    chunks = matrix.shape[1]
    size = matrix.shape[2]
    core, row_start, col_start = places()
    sources = (primal, dual)
    results = (every_primal, every_dual)
    panel, column = slice(0, wide), slice(wide, None)

    def fetch(which, chunk):
        return pltpu.make_async_copy(
            sources[which].at[pl.ds(chunk * size, size)],
            matrix.at[which, chunk],
            sems.at[which, chunk],
        )

    inputs = [
        pltpu.make_async_copy(gathered_in, gathered, in_sems.at[0]),
        pltpu.make_async_copy(other_in, other, in_sems.at[1]),
        pltpu.make_async_copy(rows_in, rows, in_sems.at[2]),
    ]
    for copy in inputs[:2]:
        copy.start()
    for which in range(2):
        for chunk in range(chunks):
            fetch(which, chunk).start()
    inputs[2].start()
    for copy in inputs[:2]:
        copy.wait()

    blocks = gathered.shape[0]
    own = other.shape[2]
    half = other.shape[1] * own
    mine_at = pl.multiple_of(core * half, half)
    other_at = pl.multiple_of((1 - core) * half, half)
    for b in range(blocks):
        lanes = slice(b * LANES, (b + 1) * LANES)
        every[pl.ds(mine_at, half), lanes] = gathered[b, :, :own, :].reshape(half, LANES)
        every[pl.ds(other_at, half), lanes] = other[b].reshape(half, LANES)
        every[wide:, lanes] = gathered[b, :, own:, :].reshape(-1, LANES)

    for which in range(2):

        @pl.loop(0, chunks)
        def _(chunk):
            fetch(which, chunk).wait()
            at = pl.multiple_of(chunk * size, size)
            results[which][panel, pl.ds(at, size)] = nt(
                every[panel, :], matrix[which, chunk]
            ).astype(jnp.bfloat16)

    inputs[2].wait()
    shift = panel_shift(parts)
    block[...] = nt(every[panel, :], every_primal[panel, :]) * nt(
        every[panel, :], every_dual[panel, :]
    ) + on_panel((wide, wide), 0, shift)
    count = rows.shape[0]
    cols = every.shape[0] - wide
    row_step = count // chunks
    col_step = cols // chunks

    def beside(chunk):
        at = pl.multiple_of(chunk * size, size)
        for which in range(2):
            results[which][column, pl.ds(at, size)] = nt(
                every[column, :], matrix[which, chunk]
            ).astype(jnp.bfloat16)
        rows_at = pl.ds(pl.multiple_of(chunk * row_step, row_step), row_step)
        row_products[rows_at, :] = nt(rows[rows_at, :], every_primal[panel, :]) * nt(
            rows[rows_at, :], every_dual[panel, :]
        )
        cols_at = pl.ds(pl.multiple_of(chunk * col_step, col_step), col_step)
        from_every = every[pl.ds(pl.multiple_of(wide + chunk * col_step, col_step), col_step), :]
        col_products[cols_at, :] = nt(from_every, every_primal[panel, :]) * nt(
            from_every, every_dual[panel, :]
        )

    factor_block(block, inverse, rest, work, beside)
    columns = col_products[...] + on_panel((cols, wide), col_start, shift)
    products = row_products[...] + on_panel((count, wide), row_start, shift)
    lower = inverse[...]
    col_factor = from_panel(nt(columns, lower, HIGHEST), col_start)
    factor = from_panel(nt(products, lower, HIGHEST), row_start)
    row_factor[...] = factor
    own_shift = jnp.sum(on_panel((count, count), 0, shift_row[...]), axis=1, keepdims=True)
    schur = nt(rows[...], every_primal[column, :]) * nt(rows[...], every_dual[column, :])
    row = lax.broadcasted_iota(jnp.int32, schur.shape, 0) + row_start
    lane = lax.broadcasted_iota(jnp.int32, schur.shape, 1) + col_start
    schur = schur + jnp.where(row == lane, jnp.broadcast_to(own_shift, schur.shape), 0.0)
    trailing[...] = schur - nt(factor, col_factor, HIGHEST)


def whole(places, gathered, other, rows, parts, shift_row, primal, dual):
    wide = PB * PANELS
    depth = primal.shape[0]
    count = rows.shape[0]
    cols = gathered.shape[1] * (gathered.shape[2] - other.shape[2])
    chunks = wide // LANES
    bf16, f32 = jnp.bfloat16, jnp.float32
    in_vmem = pl.BlockSpec(memory_space=pltpu.VMEM)
    in_place = pl.BlockSpec(memory_space=pl.ANY)
    return pl.pallas_call(
        functools.partial(whole_kernel, places),
        out_shape=(
            jax.ShapeDtypeStruct((count, cols), f32),
            jax.ShapeDtypeStruct((count, wide), f32),
        ),
        in_specs=[in_place, in_place, in_place, in_vmem, in_vmem, in_place, in_place],
        out_specs=(in_vmem, in_vmem),
        scratch_shapes=[
            pltpu.VMEM(gathered.shape, bf16),
            pltpu.VMEM(other.shape, bf16),
            pltpu.VMEM((count, depth), bf16),
            pltpu.VMEM((2, chunks, depth // chunks, depth), bf16),
            pltpu.VMEM((wide + cols, depth), bf16),
            pltpu.VMEM((wide + cols, depth), bf16),
            pltpu.VMEM((wide + cols, depth), bf16),
            pltpu.VMEM((wide, wide), f32),
            pltpu.VMEM((wide, wide), f32),
            pltpu.VMEM((wide, wide), f32),
            pltpu.VMEM((LANES, 2 * LANES), f32),
            pltpu.VMEM((count, wide), f32),
            pltpu.VMEM((cols, wide), f32),
            pltpu.SemaphoreType.DMA((2, chunks)),
            pltpu.SemaphoreType.DMA((3,)),
        ],
        compiler_params=pltpu.CompilerParams(vmem_limit_bytes=VMEM_BYTES),
        name="whole",
    )(gathered, other, rows, parts, shift_row, primal, dual)


def local(constraints, primal, dual_inv, diag_shift):
    n_row = lax.axis_size("row")
    n_col = lax.axis_size("col")
    depth, own = constraints.shape
    blocks = depth // LANES
    local_rows = own * n_col
    local_cols = own * n_row

    def places():
        col_place = lax.axis_index("col")
        return col_place % 2, lax.axis_index("row") * local_rows, col_place * local_cols

    cons = constraints.T
    cons_rows = lax.all_gather(cons, "col", axis=0, tiled=True)

    parts = cons.reshape(own, blocks, LANES).transpose(1, 0, 2)
    shift = jnp.concatenate([x.reshape(-1, LANES) for x in split_three(diag_shift)], axis=0)
    shift = jnp.pad(shift, ((0, own - shift.shape[0]), (0, 0)))
    first = jnp.concatenate([parts, jnp.broadcast_to(shift, (blocks, own, LANES))], axis=1)
    first = exchange(first, "row")
    shift = first[0, own:]

    first = first[:, :own]
    second = jnp.concatenate(
        [
            jnp.broadcast_to(first[0], (n_col, own, LANES)),
            jnp.repeat(first, n_col // n_row, axis=0),
        ],
        axis=1,
    )
    second = exchange(second, "col")

    third = lax.dynamic_slice_in_dim(second, lax.axis_index("col") % 2 * n_row, n_row, 0)
    third = exchange(jnp.broadcast_to(third, (n_row,) + third.shape), "row")
    other = lax.ppermute(third[:, :, :own], "col", [(c, c ^ 1) for c in range(n_col)])

    return whole(
        places,
        third,
        other,
        cons_rows,
        shift,
        diag_shift.reshape(1, -1),
        primal,
        dual_inv,
    )


def solution(mesh):
    return jax.shard_map(
        local,
        mesh=mesh,
        in_specs=(P(None, ("row", "col")), P(), P(), P("row")),
        out_specs=(P("row", "col"), P("row", None)),
        check_vma=False,
    )
```

```python
import functools

import jax
import jax.numpy as jnp
from jax import lax
from jax.experimental import pallas as pl
from jax.experimental.pallas import tpu as pltpu
from jax.sharding import PartitionSpec as P

PB = 256
PANELS = 2
LANES = 128
SUB = 8
HIGHEST = lax.Precision.HIGHEST

VMEM_BYTES = 60 * 1024 * 1024


def nt(left, right, precision=None):
    return lax.dot_general(
        left,
        right,
        (((1,), (1,)), ((), ())),
        precision=precision,
        preferred_element_type=jnp.float32,
    )


def dot_full(left, right):
    return jnp.dot(left, right, precision=HIGHEST, preferred_element_type=jnp.float32)


def exchange(value, axis):
    return lax.all_to_all(value, axis, split_axis=0, concat_axis=0, tiled=True)


def split_three(value):
    high = value.astype(jnp.bfloat16)
    rest = value - high.astype(jnp.float32)
    middle = rest.astype(jnp.bfloat16)
    low = (rest - middle.astype(jnp.float32)).astype(jnp.bfloat16)
    return high, middle, low


def spread_lane(value, at):
    return jnp.broadcast_to(value[:, at : at + 1], (SUB, LANES))


def spread_row(value, at):
    return jnp.broadcast_to(value[at : at + 1, :], (SUB, LANES))


def tree_sum(terms):
    while len(terms) > 1:
        paired = [a + b for a, b in zip(terms[::2], terms[1::2])]
        terms = paired + terms[len(terms) // 2 * 2 :]
    return terms[0]


def eliminate(work):
    row = lax.broadcasted_iota(jnp.int32, (SUB, LANES), 0)
    steps = LANES // SUB
    for step in range(steps):
        low = step * SUB
        here = slice(low, low + SUB)
        left = work[here, :LANES]
        right = work[here, LANES:]
        inv = [spread_lane(left, low + k) for k in range(SUB)]
        forward = [jnp.where(row == k, 1.0, 0.0) for k in range(SUB)]
        scale = None
        for i in range(SUB):
            pivot = spread_row(inv[i], i)
            recip = 1.0 / pivot
            root = lax.rsqrt(pivot)
            scale = root if scale is None else jnp.where(row == i, root, scale)
            ratio = inv[i] * recip
            below = jnp.where(row > i, ratio, 0.0)
            for k in range(i + 1):
                forward[k] = forward[k] - below * spread_row(forward[k], i)
            updated = []
            for k in range(SUB):
                if k == i:
                    updated.append(jnp.where(row == i, recip, -ratio))
                else:
                    across = spread_row(inv[k], i)
                    updated.append(
                        jnp.where(row == i, across * recip, inv[k] - ratio * across)
                    )
            inv = updated
        right_rows = [spread_row(right, k) for k in range(SUB)]
        if step + 1 < steps:
            left_rows = [spread_row(left, k) for k in range(SUB)]
            solved_left = tree_sum([inv[k] * left_rows[k] for k in range(SUB)])
            solved_right = tree_sum([inv[k] * right_rows[k] for k in range(SUB)])
            left_terms = [spread_row(solved_left, k) for k in range(SUB)]
            right_terms = [spread_row(solved_right, k) for k in range(SUB)]
            for later in range(step + 1, steps):
                there = slice(later * SUB, later * SUB + SUB)
                current = work[there, :LANES]
                weights = [spread_lane(current, low + k) for k in range(SUB)]
                work[there, :LANES] = current - tree_sum(
                    [weights[k] * left_terms[k] for k in range(SUB)]
                )
                work[there, LANES:] = work[there, LANES:] - tree_sum(
                    [weights[k] * right_terms[k] for k in range(SUB)]
                )
        work[here, LANES:] = scale * tree_sum(
            [forward[k] * right_rows[k] for k in range(SUB)]
        )


def factor_block(block, inverse, rest, work, beside):
    size = block.shape[0]
    row = lax.broadcasted_iota(jnp.int32, (LANES, LANES), 0)
    lane = lax.broadcasted_iota(jnp.int32, (LANES, LANES), 1)
    eye = jnp.where(row == lane, 1.0, 0.0).astype(jnp.float32)
    for panel in range(PANELS):
        at = slice(panel * PB, (panel + 1) * PB)
        pivot = block[at, at]
        rest[at, at] = 0.5 * (pivot + pivot.T)
        for later in range(panel + 1, PANELS):
            below = slice(later * PB, (later + 1) * PB)
            rest[at, below] = block[below, at].T
    inverse[...] = jnp.zeros_like(inverse)

    def load(low):
        work[:, :LANES] = rest[low : low + LANES, low : low + LANES]

    def update(low):
        high = low + LANES
        own = work[:, LANES:]
        if low:
            inverse[low:high, :low] = dot_full(own, inverse[low:high, :low])
        inverse[low:high, low:high] = own
        if high < size:
            upper = dot_full(own, rest[low:high, high:])
            lower = upper.T
            rest[high:, high:] = rest[high:, high:] - dot_full(lower, upper)
            inverse[high:, :high] = inverse[high:, :high] - dot_full(
                lower, inverse[low:high, :high]
            )

    @pl.loop(0, size // LANES)
    def _(block_index):
        for index in range(size // LANES):
            pl.when(block_index == index)(lambda: load(index * LANES))
        work[:, LANES:] = eye
        beside(block_index)
        eliminate(work)
        for index in range(size // LANES):
            pl.when(block_index == index)(lambda: update(index * LANES))


def panel_shift(parts):
    count = PB * PANELS // LANES
    wide = parts[...].astype(jnp.float32)
    wide = wide[:count] + wide[count : 2 * count] + wide[2 * count : 3 * count]
    return jnp.concatenate([wide[k : k + 1] for k in range(count)], axis=1)


def on_panel(shape, start, shift):
    row = lax.broadcasted_iota(jnp.int32, shape, 0) + start
    lane = lax.broadcasted_iota(jnp.int32, shape, 1)
    return jnp.where(row == lane, jnp.broadcast_to(shift, shape), 0.0)


def from_panel(rows, start):
    row = lax.broadcasted_iota(jnp.int32, rows.shape, 0) + start
    lane = lax.broadcasted_iota(jnp.int32, rows.shape, 1)
    return jnp.where(row >= lane // PB * PB, rows, 0.0)


def whole_kernel(
    places,
    gathered_in,
    other_in,
    rows_in,
    parts,
    shift_row,
    primal,
    dual,
    trailing,
    row_factor,
    gathered,
    other,
    rows,
    matrix,
    every,
    results,
    block,
    rest,
    inverse,
    work,
    row_grams,
    col_grams,
    sems,
    in_sems,
):
    wide = PB * PANELS
    chunks = matrix.shape[1]
    size = matrix.shape[2]
    core, row_start, col_start = places()
    sources = (primal, dual)
    panel, column = slice(0, wide), slice(wide, None)

    def fetch(which, chunk):
        return pltpu.make_async_copy(
            sources[which].at[pl.ds(chunk * size, size)],
            matrix.at[which, chunk],
            sems.at[which, chunk],
        )

    inputs = [
        pltpu.make_async_copy(gathered_in, gathered, in_sems.at[0]),
        pltpu.make_async_copy(other_in, other, in_sems.at[1]),
        pltpu.make_async_copy(rows_in, rows, in_sems.at[2]),
    ]
    for copy in inputs[:2]:
        copy.start()
    for which in range(2):
        for chunk in range(chunks):
            fetch(which, chunk).start()
    inputs[2].start()
    for copy in inputs[:2]:
        copy.wait()

    blocks = gathered.shape[0]
    own = other.shape[2]
    half = other.shape[1] * own
    mine_at = pl.multiple_of(core * half, half)
    other_at = pl.multiple_of((1 - core) * half, half)
    for b in range(blocks):
        lanes = slice(b * LANES, (b + 1) * LANES)
        every[pl.ds(mine_at, half), lanes] = gathered[b, :, :own, :].reshape(half, LANES)
        every[pl.ds(other_at, half), lanes] = other[b].reshape(half, LANES)
        every[wide:, lanes] = gathered[b, :, own:, :].reshape(-1, LANES)

    for which in range(2):

        @pl.loop(0, chunks)
        def _(chunk):
            fetch(which, chunk).wait()
            at = pl.multiple_of(chunk * size, size)
            results[which, panel, pl.ds(at, size)] = nt(
                every[panel, :], matrix[which, chunk]
            ).astype(jnp.bfloat16)

    inputs[2].wait()
    shift = panel_shift(parts)
    block[...] = nt(every[panel, :], results[0, panel, :]) * nt(
        every[panel, :], results[1, panel, :]
    ) + on_panel((wide, wide), 0, shift)
    count = rows.shape[0]
    cols = every.shape[0] - wide
    part = 2 * wide // chunks

    def beside(chunk):
        at = pl.multiple_of(chunk * size, size)
        for which in range(2):
            results[which, column, pl.ds(at, size)] = nt(
                every[column, :], matrix[which, chunk]
            ).astype(jnp.bfloat16)
        of, piece = chunk // 2, chunk % 2
        panel_at = pl.ds(pl.multiple_of(piece * part, part), part)
        right = results[of, panel_at, :]
        row_grams[chunk] = nt(rows[...], right)
        col_grams[chunk] = nt(every[column, :], right)

    factor_block(block, inverse, rest, work, beside)
    columns, products = [
        jnp.concatenate([grams[0] * grams[2], grams[1] * grams[3]], axis=1)
        for grams in (col_grams, row_grams)
    ]
    columns = columns + on_panel((cols, wide), col_start, shift)
    products = products + on_panel((count, wide), row_start, shift)
    lower = inverse[...]
    col_factor = from_panel(nt(columns, lower, HIGHEST), col_start)
    factor = from_panel(nt(products, lower, HIGHEST), row_start)
    row_factor[...] = factor
    own_shift = jnp.sum(on_panel((count, count), 0, shift_row[...]), axis=1, keepdims=True)
    schur = nt(rows[...], results[0, column, :]) * nt(rows[...], results[1, column, :])
    row = lax.broadcasted_iota(jnp.int32, schur.shape, 0) + row_start
    lane = lax.broadcasted_iota(jnp.int32, schur.shape, 1) + col_start
    schur = schur + jnp.where(row == lane, jnp.broadcast_to(own_shift, schur.shape), 0.0)
    trailing[...] = schur - nt(factor, col_factor, HIGHEST)


def whole(places, gathered, other, rows, parts, shift_row, primal, dual):
    wide = PB * PANELS
    depth = primal.shape[0]
    count = rows.shape[0]
    cols = gathered.shape[1] * (gathered.shape[2] - other.shape[2])
    chunks = wide // LANES
    bf16, f32 = jnp.bfloat16, jnp.float32
    in_vmem = pl.BlockSpec(memory_space=pltpu.VMEM)
    in_place = pl.BlockSpec(memory_space=pl.ANY)
    return pl.pallas_call(
        functools.partial(whole_kernel, places),
        out_shape=(
            jax.ShapeDtypeStruct((count, cols), f32),
            jax.ShapeDtypeStruct((count, wide), f32),
        ),
        in_specs=[in_place, in_place, in_place, in_vmem, in_vmem, in_place, in_place],
        out_specs=(in_vmem, in_vmem),
        scratch_shapes=[
            pltpu.VMEM(gathered.shape, bf16),
            pltpu.VMEM(other.shape, bf16),
            pltpu.VMEM((count, depth), bf16),
            pltpu.VMEM((2, chunks, depth // chunks, depth), bf16),
            pltpu.VMEM((wide + cols, depth), bf16),
            pltpu.VMEM((2, wide + cols, depth), bf16),
            pltpu.VMEM((wide, wide), f32),
            pltpu.VMEM((wide, wide), f32),
            pltpu.VMEM((wide, wide), f32),
            pltpu.VMEM((LANES, 2 * LANES), f32),
            pltpu.VMEM((chunks, count, 2 * wide // chunks), f32),
            pltpu.VMEM((chunks, cols, 2 * wide // chunks), f32),
            pltpu.SemaphoreType.DMA((2, chunks)),
            pltpu.SemaphoreType.DMA((3,)),
        ],
        compiler_params=pltpu.CompilerParams(vmem_limit_bytes=VMEM_BYTES),
        name="whole",
    )(gathered, other, rows, parts, shift_row, primal, dual)


def local(constraints, primal, dual_inv, diag_shift):
    n_row = lax.axis_size("row")
    n_col = lax.axis_size("col")
    depth, own = constraints.shape
    blocks = depth // LANES
    local_rows = own * n_col
    local_cols = own * n_row

    def places():
        col_place = lax.axis_index("col")
        return col_place % 2, lax.axis_index("row") * local_rows, col_place * local_cols

    cons = constraints.T
    cons_rows = lax.all_gather(cons, "col", axis=0, tiled=True)

    parts = cons.reshape(own, blocks, LANES).transpose(1, 0, 2)
    shift = jnp.concatenate([x.reshape(-1, LANES) for x in split_three(diag_shift)], axis=0)
    shift = jnp.pad(shift, ((0, own - shift.shape[0]), (0, 0)))
    first = jnp.concatenate([parts, jnp.broadcast_to(shift, (blocks, own, LANES))], axis=1)
    first = exchange(first, "row")
    shift = first[0, own:]

    first = first[:, :own]
    second = jnp.concatenate(
        [
            jnp.broadcast_to(first[0], (n_col, own, LANES)),
            jnp.repeat(first, n_col // n_row, axis=0),
        ],
        axis=1,
    )
    second = exchange(second, "col")

    third = lax.dynamic_slice_in_dim(second, lax.axis_index("col") % 2 * n_row, n_row, 0)
    third = exchange(jnp.broadcast_to(third, (n_row,) + third.shape), "row")
    other = lax.ppermute(third[:, :, :own], "col", [(c, c ^ 1) for c in range(n_col)])

    return whole(
        places,
        third,
        other,
        cons_rows,
        shift,
        diag_shift.reshape(1, -1),
        primal,
        dual_inv,
    )


def solution(mesh):
    return jax.shard_map(
        local,
        mesh=mesh,
        in_specs=(P(None, ("row", "col")), P(), P(), P("row")),
        out_specs=(P("row", "col"), P("row", None)),
        check_vma=False,
    )
```
